32 devices in a mesh: chan: 16 (over z, y, core), tm: 2 (over x).
Axes of the slice: x: 2, y: 2, z: 4, core: 2. Of those that a mesh axis runs over, the one named last changes fastest.
Arguments:
- traces: float32 [8, 1024, 1500], P('tm', 'chan'), may hold values from -6 to 6
- plan: int32 [16, 3], P('chan'), may hold values 0 or 1
- dead_channels: int32 [96], replicated, may hold values from 0 to 1023
Outputs:
- correlations: float32 [16, 64, 3, 64, 129], P('chan', 'tm')
The draws below stay inside these ranges and needn't reach their ends.
Inputs may be any that keep to these rules, and one draw needn't show every extreme that they name: `dead_channels`: entries may repeat.
All inputs are finite; a program needn't handle non-finite values. No bound on the sum of `plan` on one device may be relied on, other than what follows from the above.
Results may differ from the reference program's by a relative error of at most 0.0085.
Values may be sent and summed in bfloat16 or wider, within the bound.
No kernel may reach another device: no remote copies, remote signals or barrier semaphores. Data moves between devices by JAX's collectives and lax.ppermute only.
A program may use at most 64 MiB of HBM per device.

```python
import math
import jax
import jax.numpy as jnp
from jax import lax

CH = 64
WIN_DEV = 4
SAMPLES = 1500
BINS = 128
HALF_LAG = 64
NDEAD = 96
OFFS = 3
LAGS = 129
BLOCKS = 16
CHANNELS = 1024
WINDOWS = 8
N_TM = 2


def with_ends(drawn, stream_key, low, largest):
    longest = drawn.shape.index(max(drawn.shape))
    spots = []
    for shift in (0, 1):
        where = [jax.random.randint(jax.random.fold_in(stream_key, axis), (), 0, length) for axis, length in enumerate(drawn.shape)]
        where[longest] = (where[longest] + shift) % drawn.shape[longest]
        spots.append(tuple(where))
    return drawn.at[spots[0]].set(low).at[spots[1]].set(largest)


def block_levels(stream_key, shape, shards, smallest, largest):
    factor_of, own = 1.0, jax.random.fold_in(stream_key, 6)
    for dim, parts in shards:
        heights = jnp.exp(jax.random.uniform(jax.random.fold_in(own, dim), (parts,), jnp.float32, smallest / len(shards), largest / len(shards)))
        factor_of = factor_of * jnp.repeat(heights, shape[dim] // parts).reshape([-1 if axis == dim else 1 for axis in range(len(shape))])
    return factor_of


def scatter_about(stream_key, dims, scale, most, cuts=(), kind=jnp.bfloat16):
    result = scale * jax.random.normal(stream_key, dims, jnp.float32)
    if cuts:
        result = result * block_levels(stream_key, dims, cuts, -0.22, 0.18)
    return jnp.clip(result, -most, most).astype(kind)


def setup_inputs(seed: int = 0) -> dict:
    arg_keys = jax.random.split(jax.random.key(seed), 4)
    traces = scatter_about(arg_keys[0], (WINDOWS, CHANNELS, SAMPLES), 1.0, 6.0, ((0, 2), (1, 16)), jnp.float32)
    plan = with_ends((jax.random.randint(arg_keys[1], (BLOCKS, OFFS), 0, 4) < 3).astype(jnp.int32), jax.random.fold_in(arg_keys[1], 1), 0, 1)
    dead_channels = with_ends(jax.random.randint(arg_keys[2], (NDEAD,), 0, CHANNELS), jax.random.fold_in(arg_keys[2], 1), 0, CHANNELS - 1).astype(jnp.int32)
    return dict(traces=traces, plan=plan, dead_channels=dead_channels)


WATER_LEVEL = 0.1
EPSILON = 1e-06

def dft_table(samples, freq_bins):
    frequency = jnp.arange(1, freq_bins + 1, dtype=jnp.int32)
    sample_index = jnp.arange(samples, dtype=jnp.int32)
    phases = jnp.mod(sample_index[:, None] * frequency[None, :], samples).astype(jnp.float32) * (2.0 * math.pi / samples)
    return jnp.concatenate([jnp.cos(phases), -jnp.sin(phases)], axis=1)

def lag_table(samples, freq_bins, half_lag, scale):
    frequency = jnp.arange(1, freq_bins + 1, dtype=jnp.int32)
    lag_index = jnp.arange(-half_lag, half_lag + 1, dtype=jnp.int32)
    phases = jnp.mod(frequency[:, None] * lag_index[None, :], samples).astype(jnp.float32) * (2.0 * math.pi / samples)
    return jnp.concatenate([jnp.cos(phases), -jnp.sin(phases)], axis=0) * scale

def whiten(raw_traces, dft_matrix, live_mask, freq_bins):
    windows, channels, samples = raw_traces.shape
    spectra = jnp.dot(raw_traces.reshape(windows * channels, samples), dft_matrix, precision=lax.Precision.HIGHEST)
    spectra = spectra.reshape(windows, channels, 2 * freq_bins)
    real_part = spectra[..., :freq_bins]
    imag_part = spectra[..., freq_bins:]
    powers = real_part * real_part + imag_part * imag_part
    mean_power = lax.optimization_barrier(jnp.mean(powers, axis=-1, keepdims=True))
    denominator = jnp.sqrt(powers + WATER_LEVEL * mean_power + EPSILON)
    whitened = jnp.concatenate([real_part / denominator, imag_part / denominator], axis=-1)
    return whitened * live_mask[None, :, None]

def cross_spectra(own_block, far_block, freq_bins):
    own_real = own_block[:, :, None, :freq_bins]
    own_imag = own_block[:, :, None, freq_bins:]
    far_real = far_block[:, None, :, :freq_bins]
    far_imag = far_block[:, None, :, freq_bins:]
    real_part = lax.optimization_barrier(jnp.sum(own_real * far_real + own_imag * far_imag, axis=0))
    imag_part = lax.optimization_barrier(jnp.sum(own_imag * far_real - own_real * far_imag, axis=0))
    return jnp.concatenate([real_part, imag_part], axis=-1)

def reference(traces, plan, dead_channels):
    dft_matrix = dft_table(SAMPLES, BINS)
    chan_ids = jnp.arange(CHANNELS, dtype=jnp.int32)
    live_mask = 1.0 - jnp.any(dead_channels[:, None] == chan_ids[None, :], axis=0).astype(jnp.float32)

    def whiten_window(window_traces):
        return whiten(window_traces[None], dft_matrix, live_mask, BINS)[0]
    spectra = lax.map(whiten_window, traces)
    blocks = spectra.reshape(N_TM, WIN_DEV, BLOCKS, CH, 2 * BINS)
    lag_matrix = lag_table(SAMPLES, BINS, HALF_LAG, 1.0 / math.sqrt(BINS * WINDOWS))
    upper_mask = (jnp.arange(CH)[None, :] > jnp.arange(CH)[:, None]).astype(jnp.float32)

    def one_block(block_index):
        own_all = lax.dynamic_index_in_dim(blocks, block_index, axis=2, keepdims=False)
        far_all = []
        for offset in range(OFFS):
            partner = jnp.mod(block_index - offset, BLOCKS).astype(jnp.int32)
            far_all.append(lax.dynamic_index_in_dim(blocks, partner, axis=2, keepdims=False))
        total = jnp.zeros((CH, OFFS, CH, LAGS), jnp.float32)
        for group in range(N_TM):
            columns = []
            for offset in range(OFFS):
                spectrum = cross_spectra(own_all[group], far_all[offset][group], BINS)
                weight = plan[block_index, offset].astype(jnp.float32)
                if offset == 0:
                    spectrum = spectrum * (upper_mask * weight)[:, :, None]
                else:
                    spectrum = spectrum * weight
                columns.append(spectrum)
            stacked = jnp.stack(columns, axis=1)
            lagged = jnp.dot(stacked.reshape(-1, 2 * BINS), lag_matrix, precision=lax.Precision.HIGHEST)
            total = total + lagged.reshape(CH, OFFS, CH, LAGS).astype(jnp.bfloat16).astype(jnp.float32)
        return total
    return lax.map(one_block, jnp.arange(BLOCKS, dtype=jnp.int32))
```

```python
import functools
import math

import jax
import jax.numpy as jnp
import ml_dtypes
import numpy as np
from jax import lax
from jax.experimental import pallas as pl
from jax.experimental.pallas import tpu as pltpu
from jax.sharding import PartitionSpec as P

BINS = 128
HALF_LAG = 64
OFFS = 3
LAGS = 2 * HALF_LAG + 1
WATER_LEVEL = 0.1
EPSILON = 1e-06

LANES = 128
RUN = 16
GROUPS = BINS // RUN
STEP = 8

F32 = jnp.float32
BF16 = jnp.bfloat16


def dft_tables(samples):
    phase = (np.arange(samples)[:, None] * np.arange(1, BINS + 1)[None, :]) % samples
    phase = phase * (2.0 * math.pi / samples)
    table = np.concatenate([np.cos(phase), -np.sin(phase)], axis=1)
    high = table.astype(ml_dtypes.bfloat16)
    low = (table - high.astype(np.float64)).astype(ml_dtypes.bfloat16)
    return high, low


def lag_table(samples, total_windows):
    lags = np.arange(-HALF_LAG, HALF_LAG + 1)
    phase = (np.arange(1, BINS + 1)[:, None] * lags[None, :]) % samples
    phase = phase * (2.0 * math.pi / samples)
    table = np.concatenate([np.cos(phase), -np.sin(phase)], axis=0)
    return (table / math.sqrt(BINS * total_windows)).astype(ml_dtypes.bfloat16)


def spectra_kernel(first_ref, dead_ref, trace_ref, high_ref, low_ref, out_ref):
    windows, channels, samples = trace_ref.shape
    traces = trace_ref[...].reshape(windows * channels, samples)
    high = traces.astype(BF16)
    low = (traces - high.astype(F32)).astype(BF16)
    dot = functools.partial(jnp.dot, preferred_element_type=F32)
    raw = dot(high, high_ref[...]) + dot(low, high_ref[...]) + dot(high, low_ref[...])
    ids = first_ref[0] + lax.broadcasted_iota(jnp.int32, (channels, 1), 0)
    dead = jnp.where(ids == dead_ref[...], 1.0, 0.0)
    live = 1.0 - jnp.max(dead, axis=1, keepdims=True)
    parts = []
    for window in range(windows):
        rows = slice(window * channels, (window + 1) * channels)
        real, imag = raw[rows, :BINS], raw[rows, BINS:]
        power = real * real + imag * imag
        mean = jnp.sum(power, axis=1, keepdims=True) * (1.0 / BINS)
        factor = lax.rsqrt(power + WATER_LEVEL * mean + EPSILON) * live
        parts += [real * factor, imag * factor]
    run_of = lax.broadcasted_iota(jnp.int32, (1, LANES), 1) // RUN
    for bit in (1, 2, 4):
        keep = (run_of & bit) == 0
        for index in range(len(parts)):
            if index & bit:
                continue
            first, second = parts[index], parts[index | bit]
            parts[index] = jnp.where(keep, first, pltpu.roll(second, bit * RUN, 1))
            parts[index | bit] = jnp.where(keep, pltpu.roll(first, LANES - bit * RUN, 1), second)
    for group, part in enumerate(parts):
        out_ref[:, group * LANES : (group + 1) * LANES] = part.astype(BF16)


def block_spectra(traces, dead_channels, first_channel):
    windows, channels, samples = traces.shape
    assert 2 * windows == LANES // RUN and GROUPS == 2 * windows
    high, low = dft_tables(samples)
    vmem = pl.BlockSpec(memory_space=pltpu.VMEM)
    return pl.pallas_call(
        spectra_kernel,
        out_shape=jax.ShapeDtypeStruct((channels, GROUPS * LANES), BF16),
        in_specs=[pl.BlockSpec(memory_space=pltpu.SMEM), vmem, vmem, vmem, vmem],
        out_specs=vmem,
        name="spectra",
    )(first_channel, dead_channels[None, :], traces, jnp.asarray(high), jnp.asarray(low))


def correlation_kernel(offsets, sources, share, rank_ref, plan_ref, lag_ref, *refs):
    own_refs, refs = refs[:sources], refs[sources:]
    far_refs, refs = refs[: sources * len(offsets)], refs[sources * len(offsets) :]
    out_ref, real_ref, imag_ref, far_ref, cross_ref, lagged_ref, sems = refs[-7:]
    channels = own_refs[0].shape[0]
    columns = len(offsets) * channels
    pairs = sources // 2
    rank = rank_ref[0]
    first_row = rank * share

    run_of = lax.broadcasted_iota(jnp.int32, (1, LANES), 1) // RUN
    even = (run_of & 1) == 0
    for source, own_ref in enumerate(own_refs):
        for group in range(GROUPS):
            lanes = pl.ds(((source // 2) * GROUPS + group) * 2 * LANES + (source % 2) * LANES, LANES)
            value = own_ref[:, group * LANES : (group + 1) * LANES].astype(F32)
            real_ref[:, lanes] = value
            left, right = pltpu.roll(value, LANES - RUN, 1), pltpu.roll(value, RUN, 1)
            imag_ref[:, lanes] = jnp.where(even, left, -right)
    for place in range(len(offsets)):
        for source in range(sources):
            far = far_refs[place * sources + source]
            for group in range(GROUPS):
                far_ref[
                    (source // 2) * GROUPS + group,
                    place * channels : (place + 1) * channels,
                    (source % 2) * LANES : (source % 2 + 1) * LANES,
                ] = far[:, group * LANES : (group + 1) * LANES]

    diagonal = (
        lax.broadcasted_iota(jnp.int32, (RUN, 2 * LANES), 1) % RUN
        == lax.broadcasted_iota(jnp.int32, (RUN, 2 * LANES), 0)
    )
    column = lax.broadcasted_iota(jnp.int32, (1, columns), 1)
    weight = jnp.full((1, columns), plan_ref[0, offsets[-1]].astype(F32))
    for place in range(len(offsets) - 1):
        here = plan_ref[0, offsets[place]].astype(F32)
        weight = jnp.where(column // channels == place, here, weight)
    lags = lag_ref[...]

    def copy(step):
        return pltpu.make_async_copy(
            lagged_ref.at[step],
            out_ref.at[0, pl.ds(step * STEP, STEP), pl.ds(offsets[0], len(offsets))],
            sems.at[step],
        )

    def one_step(step, carry):
        for group in range(GROUPS):
            total = None
            for pair in range(pairs):
                blocks = []
                lanes = pl.ds((pair * GROUPS + group) * 2 * LANES, 2 * LANES)
                for row in range(STEP):
                    for ref in (real_ref, imag_ref):
                        one = ref[pl.ds(first_row + step * STEP + row, 1), lanes]
                        spread = jnp.broadcast_to(one, (RUN, 2 * LANES))
                        blocks.append(jnp.where(diagonal, spread, 0.0).astype(BF16))
                near = jnp.concatenate(blocks, axis=0)
                term = lax.dot_general(
                    near,
                    far_ref[pair * GROUPS + group],
                    (((1,), (1,)), ((), ())),
                    preferred_element_type=F32,
                )
                total = term if total is None else total + term
            for row in range(STEP):
                scale = weight
                if offsets[0] == 0:
                    above = column > first_row + step * STEP + row
                    scale = jnp.where(jnp.logical_or(above, column >= channels), weight, 0.0)
                for part in range(2):
                    at = (2 * row + part) * RUN
                    cross_ref[row, part * BINS + group * RUN : part * BINS + (group + 1) * RUN, :] = (
                        total[at : at + RUN] * scale
                    ).astype(BF16)
        for row in range(STEP):
            lagged = lax.dot_general(
                cross_ref[row], lags, (((0,), (0,)), ((), ())), preferred_element_type=F32
            )
            for place in range(len(offsets)):
                lagged_ref[step, row, place] = lagged[place * channels : (place + 1) * channels]
        copy(step).start()
        return carry

    steps = share // STEP
    lax.fori_loop(0, steps, one_step, 0)
    for step in range(steps):
        copy(step).wait()


def correlate(offsets, rank, plan, samples, own, far, share, total_windows, previous=None):
    sources = len(own)
    channels = own[0].shape[0]
    count = len(offsets)
    pairs = sources // 2
    vmem = pl.BlockSpec(memory_space=pltpu.VMEM)
    smem = pl.BlockSpec(memory_space=pltpu.SMEM)
    hbm = pl.BlockSpec(memory_space=pl.ANY)
    arrays = [rank, plan, jnp.asarray(lag_table(samples, total_windows)), *own, *far]
    in_specs = [smem, smem] + [vmem] * (len(arrays) - 2)
    aliases = {}
    if previous is not None:
        aliases = {len(arrays): 0}
        arrays.append(previous)
        in_specs.append(hbm)
    steps = share // STEP
    return pl.pallas_call(
        functools.partial(correlation_kernel, offsets, sources, share),
        out_shape=jax.ShapeDtypeStruct((1, share, OFFS, channels, LAGS), F32),
        in_specs=in_specs,
        out_specs=hbm,
        scratch_shapes=[
            pltpu.VMEM((channels, pairs * GROUPS * 2 * LANES), F32),
            pltpu.VMEM((channels, pairs * GROUPS * 2 * LANES), F32),
            pltpu.VMEM((pairs * GROUPS, count * channels, 2 * LANES), BF16),
            pltpu.VMEM((STEP, 2 * BINS, count * channels), BF16),
            pltpu.VMEM((steps, STEP, count, channels, LAGS), F32),
            pltpu.SemaphoreType.DMA((steps,)),
        ],
        input_output_aliases=aliases,
        cost_estimate=pl.CostEstimate(
            flops=2 * share * 2 * BINS * 2 * LANES * pairs * channels * count,
            bytes_accessed=share * count * channels * 2 * LANES * 4,
            transcendentals=0,
        ),
        name="correlate_" + "_".join(str(offset) for offset in offsets),
    )(*arrays)


def moved(value, blocks, ranks):
    block_count, rank_count = lax.axis_size("chan"), lax.axis_size("tm")
    pairs = []
    for block in range(block_count):
        for rank in range(rank_count):
            to = ((block + blocks) % block_count) * rank_count + (rank + ranks) % rank_count
            pairs.append((block * rank_count + rank, to))
    return lax.ppermute(value, ("chan", "tm"), pairs)


def shards(traces, plan, dead_channels):
    windows, channels, samples = traces.shape
    ranks = lax.axis_size("tm")
    share = channels // ranks
    assert ranks % 2 == 0 and share % STEP == 0
    first_channel = (lax.axis_index("chan") * channels).astype(jnp.int32).reshape(1)
    rank = lax.axis_index("tm").astype(jnp.int32).reshape(1)
    mine = block_spectra(traces, dead_channels, first_channel)
    blocks = [
        [mine if (offset, step) == (0, 0) else moved(mine, offset, step) for step in range(ranks)]
        for offset in range(OFFS)
    ]
    own = blocks[0]
    run = functools.partial(
        correlate,
        rank=rank,
        plan=plan,
        samples=samples,
        own=own,
        share=share,
        total_windows=windows * ranks,
    )
    result = run((0,), far=own)
    return run((1, 2), far=blocks[1] + blocks[2], previous=result)


def solution(mesh):
    in_specs = (P("tm", "chan", None), P("chan", None), P())
    out_specs = P("chan", "tm", None, None, None)
    return jax.shard_map(shards, mesh=mesh, in_specs=in_specs, out_specs=out_specs, check_vma=False)
```

```python
import functools
import math

import jax
import jax.numpy as jnp
import ml_dtypes
import numpy as np
from jax import lax
from jax.experimental import pallas as pl
from jax.experimental.pallas import tpu as pltpu
from jax.sharding import PartitionSpec as P

BINS = 128
HALF_LAG = 64
OFFS = 3
LAGS = 2 * HALF_LAG + 1
WATER_LEVEL = 0.1
EPSILON = 1e-06

LANES = 128
RUN = 16
GROUPS = BINS // RUN
STEP = 16
BATCH = 8
SEGMENT = 256
VMEM_LIMIT = 24 << 20
MERGED = False

F32 = jnp.float32
BF16 = jnp.bfloat16


def dft_tables(samples):
    bins = np.arange(1, BINS + 1)[None, :]
    phase = np.arange(SEGMENT)[:, None] * bins % samples * (2.0 * math.pi / samples)
    table = np.concatenate([np.cos(phase), -np.sin(phase)], axis=1)
    high = table.astype(ml_dtypes.bfloat16)
    low = (table - high.astype(np.float64)).astype(ml_dtypes.bfloat16)
    starts = np.arange(0, samples, SEGMENT)[:, None]
    turn = starts * bins % samples * (2.0 * math.pi / samples)
    turns = np.concatenate([np.cos(turn), -np.sin(turn)], axis=1).astype(np.float32)
    return high, low, turns


def lag_table(samples, total_windows):
    lags = np.arange(-HALF_LAG, HALF_LAG + 1)
    phase = (np.arange(1, BINS + 1)[:, None] * lags[None, :]) % samples
    phase = phase * (2.0 * math.pi / samples)
    table = np.concatenate([np.cos(phase), -np.sin(phase)], axis=0)
    return (table / math.sqrt(BINS * total_windows)).astype(ml_dtypes.bfloat16)


def spectra_kernel(first_ref, *refs):
    hbm, (out_ref, weight_ref, lag_ref), places, (tail_ref, sems) = refs[:7], refs[7:10], refs[10:16], refs[16:]
    places = (*places, lag_ref)
    trace_hbm, held_ref = hbm[0], places[0]
    dead_ref, plan_ref, high_ref, low_ref, turn_ref = places[1:6]
    windows, channels, samples = trace_hbm.shape

    def copy(window):
        return pltpu.make_async_copy(trace_hbm.at[window], held_ref.at[window], sems.at[window])

    small = [
        pltpu.make_async_copy(source, place, sems.at[windows + index])
        for index, (source, place) in enumerate(zip(hbm[1:], places[1:], strict=True))
    ]
    for one in (small[2], small[3]):
        one.start()
    for window in range(windows):
        copy(window).start()
    for one in (*small[:2], *small[4:]):
        one.start()
    dot = functools.partial(jnp.dot, preferred_element_type=F32)
    segments = pl.cdiv(samples, SEGMENT)
    last = samples - (segments - 1) * SEGMENT
    tail_ref[...] = jnp.zeros_like(tail_ref)
    small[2].wait()
    small[3].wait()
    high_table, low_table = high_ref[...], low_ref[...]
    reals, imags = [], []
    live = None
    for window in range(windows):
        copy(window).wait()
        tail_ref[:, :last] = held_ref[window, :, samples - last : samples]
        highs, lows = [], []
        for segment in range(segments):
            if segment == segments - 1:
                piece = tail_ref[...]
            else:
                piece = held_ref[window, :, segment * SEGMENT : (segment + 1) * SEGMENT]
            highs.append(piece.astype(BF16))
            lows.append((piece - highs[-1].astype(F32)).astype(BF16))
        high = jnp.concatenate(highs, axis=0)
        low = jnp.concatenate(lows, axis=0)
        all_raw = dot(high, high_table) + dot(low, high_table) + dot(high, low_table)
        if window == 0:
            for one in (*small[:2], *small[4:]):
                one.wait()
            ids = first_ref[0] + lax.broadcasted_iota(jnp.int32, (channels, 1), 0)
            dead = jnp.where(ids == dead_ref[...], 1.0, 0.0)
            live = 1.0 - jnp.max(dead, axis=1, keepdims=True)
            weight_ref[...] = jnp.zeros_like(weight_ref)
            for offset in range(OFFS):
                weight = plan_ref[:, offset : offset + 1].astype(F32)
                weight_ref[offset : offset + 1, :] = jnp.broadcast_to(weight, (1, LANES))
        real = imag = None
        for segment in range(segments):
            raw = all_raw[segment * channels : (segment + 1) * channels]
            if segment == 0:
                real, imag = raw[:, :BINS], raw[:, BINS:]
            else:
                cosine = turn_ref[segment : segment + 1, :BINS]
                sine = turn_ref[segment : segment + 1, BINS:]
                real += raw[:, :BINS] * cosine - raw[:, BINS:] * sine
                imag += raw[:, BINS:] * cosine + raw[:, :BINS] * sine
        power = real * real + imag * imag
        mean = jnp.sum(power, axis=1, keepdims=True) * (1.0 / BINS)
        factor = lax.rsqrt(power + WATER_LEVEL * mean + EPSILON) * live
        reals.append(real * factor)
        imags.append(imag * factor)
    parts = reals + imags
    run_of = lax.broadcasted_iota(jnp.int32, (1, LANES), 1) // RUN
    for bit in (1, 2, 4):
        keep = (run_of & bit) == 0
        for index in range(len(parts)):
            if index & bit:
                continue
            first, second = parts[index], parts[index | bit]
            parts[index] = jnp.where(keep, first, pltpu.roll(second, bit * RUN, 1))
            parts[index | bit] = jnp.where(keep, pltpu.roll(first, LANES - bit * RUN, 1), second)
    for group, part in enumerate(parts):
        out_ref[:, group * LANES : (group + 1) * LANES] = part.astype(BF16)


def block_spectra(traces, dead_channels, plan, first_channel, total_windows):
    windows, channels, samples = traces.shape
    assert 2 * windows == LANES // RUN and GROUPS == 2 * windows
    high, low, turns = (jnp.asarray(table) for table in dft_tables(samples))
    lags = jnp.asarray(lag_table(samples, total_windows))
    arrays = [traces, dead_channels[None, :], plan, high, low, turns, lags]
    arrays = [pltpu.with_memory_space_constraint(array, pltpu.HBM) for array in arrays]
    vmem = pl.BlockSpec(memory_space=pltpu.VMEM)
    return pl.pallas_call(
        spectra_kernel,
        out_shape=[
            jax.ShapeDtypeStruct((channels, GROUPS * LANES), BF16),
            jax.ShapeDtypeStruct((8, LANES), F32),
            jax.ShapeDtypeStruct(lags.shape, lags.dtype),
        ],
        in_specs=[pl.BlockSpec(memory_space=pltpu.SMEM)]
        + [pl.BlockSpec(memory_space=pltpu.HBM)] * len(arrays),
        out_specs=[vmem] * 3,
        scratch_shapes=[pltpu.VMEM(array.shape, array.dtype) for array in arrays[:-1]]
        + [
            pltpu.VMEM((channels, SEGMENT), F32),
            pltpu.SemaphoreType.DMA((windows + len(arrays) - 1,)),
        ],
        compiler_params=pltpu.CompilerParams(vmem_limit_bytes=VMEM_LIMIT),
        name="spectra",
    )(first_channel, *arrays)


def correlation_kernel(offsets, sources, share, step_rows, rank_ref, weight_ref, lag_ref, *refs):
    own_refs, refs = refs[:sources], refs[sources:]
    far_refs, refs = refs[: sources * len(offsets)], refs[sources * len(offsets) :]
    out_ref, near_ref, far_ref, cross_ref, lagged_ref, sems = refs[-6:]
    channels = own_refs[0].shape[0]
    columns = len(offsets) * channels
    pairs = sources // 2
    first_row = rank_ref[0] * share

    def lanes_of(source, group):
        start = ((source // 2) * GROUPS + group) * 2 * LANES + (source % 2) * LANES
        return slice(start, start + LANES)

    held_first = first_row
    for source, own_ref in enumerate(own_refs):
        for group in range(GROUPS):
            at = slice(group * LANES, (group + 1) * LANES)
            if share % 16 == 0:
                value = own_ref[pl.ds(pl.multiple_of(first_row, share), share), at]
                held_first = 0
            else:
                value = own_ref[:, at]
            near_ref[:, lanes_of(source, group)] = value.astype(F32)
    sign = jnp.where(lax.broadcasted_iota(jnp.int32, (1, LANES), 1) < LANES // 2, -1.0, 1.0)
    for place, offset in enumerate(offsets):
        weight = weight_ref[offset : offset + 1, :]
        turned_weight = weight * sign
        rows = slice(place * channels, (place + 1) * channels)
        turned_rows = slice(columns + place * channels, columns + (place + 1) * channels)
        for source in range(sources):
            far = far_refs[place * sources + source]
            lanes = slice((source % 2) * LANES, (source % 2 + 1) * LANES)
            for group in range(GROUPS):
                value = far[:, group * LANES : (group + 1) * LANES].astype(F32)
                turned = pltpu.roll(value, LANES // 2, 1) * turned_weight
                slot = (source // 2) * GROUPS + group
                far_ref[slot, rows, lanes] = (value * weight).astype(BF16)
                far_ref[slot, turned_rows, lanes] = turned.astype(BF16)

    diagonal = (
        lax.broadcasted_iota(jnp.int32, (RUN, 2 * LANES), 1) % RUN
        == lax.broadcasted_iota(jnp.int32, (RUN, 2 * LANES), 0)
    )
    column = lax.broadcasted_iota(jnp.int32, (1, 2 * columns), 1) % channels
    lags = lag_ref[...]

    batch = min(BATCH, step_rows)

    def copy(index):
        return pltpu.make_async_copy(
            lagged_ref.at[index],
            out_ref.at[0, pl.ds(index * batch, batch), pl.ds(offsets[0], len(offsets))],
            sems.at[index],
        )

    def one_step(step, carry):
        for group in range(GROUPS):
            total = None
            for pair in range(pairs):
                blocks = []
                slot = pair * GROUPS + group
                lanes = slice(slot * 2 * LANES, (slot + 1) * 2 * LANES)
                for row in range(step_rows):
                    one = near_ref[pl.ds(held_first + step * step_rows + row, 1), lanes]
                    spread = jnp.broadcast_to(one, (RUN, 2 * LANES))
                    blocks.append(jnp.where(diagonal, spread, 0.0).astype(BF16))
                term = lax.dot_general(
                    jnp.concatenate(blocks, axis=0),
                    far_ref[slot],
                    (((1,), (1,)), ((), ())),
                    preferred_element_type=F32,
                )
                total = term if total is None else total + term
            for row in range(step_rows):
                value = total[row * RUN : (row + 1) * RUN]
                if offsets[0] == 0:
                    value = jnp.where(column > first_row + step * step_rows + row, value, 0.0)
                cross_ref[row, group * RUN : (group + 1) * RUN, :] = value.astype(BF16)
        for start in range(0, step_rows, batch):
            sides = []
            for row in range(start, start + batch):
                cross = cross_ref[row].T
                sides.append(jnp.concatenate([cross[:columns], cross[columns:]], axis=1))
            lagged = jnp.dot(jnp.concatenate(sides, axis=0), lags, preferred_element_type=F32)
            index = (step * step_rows + start) // batch
            lagged_ref[index] = lagged.reshape(batch, len(offsets), channels, LAGS)
            copy(index).start()
        return carry

    lax.fori_loop(0, share // step_rows, one_step, 0)
    for index in range(share // batch):
        copy(index).wait()


def correlate(offsets, rank, weights, lags, own, far, share, previous=None):
    sources = len(own)
    channels = own[0].shape[0]
    count = len(offsets)
    pairs = sources // 2
    vmem = pl.BlockSpec(memory_space=pltpu.VMEM)
    smem = pl.BlockSpec(memory_space=pltpu.SMEM)
    hbm = pl.BlockSpec(memory_space=pltpu.HBM)
    arrays = [rank, weights, lags, *own, *far]
    in_specs = [smem] + [vmem] * (len(arrays) - 1)
    aliases = {}
    if previous is not None:
        aliases = {len(arrays): 0}
        arrays.append(previous)
        in_specs.append(hbm)
    step_rows = min(STEP, share)
    batch = min(BATCH, step_rows)
    held = share if share % 16 == 0 else channels
    return pl.pallas_call(
        functools.partial(correlation_kernel, offsets, sources, share, step_rows),
        out_shape=jax.ShapeDtypeStruct((1, share, OFFS, channels, LAGS), F32),
        in_specs=in_specs,
        out_specs=hbm,
        scratch_shapes=[
            pltpu.VMEM((held, pairs * GROUPS * 2 * LANES), F32),
            pltpu.VMEM((pairs * GROUPS, 2 * count * channels, 2 * LANES), BF16),
            pltpu.VMEM((step_rows, BINS, 2 * count * channels), BF16),
            pltpu.VMEM((share // batch, batch, count, channels, LAGS), F32),
            pltpu.SemaphoreType.DMA((share // batch,)),
        ],
        compiler_params=pltpu.CompilerParams(vmem_limit_bytes=VMEM_LIMIT),
        input_output_aliases=aliases,
        cost_estimate=pl.CostEstimate(
            flops=2 * share * 2 * BINS * 2 * LANES * pairs * channels * count,
            bytes_accessed=share * count * channels * 2 * LANES * 4,
            transcendentals=0,
        ),
        name="correlate_" + "_".join(str(offset) for offset in offsets),
    )(*arrays)


def moved(value, blocks, ranks):
    block_count, rank_count = lax.axis_size("chan"), lax.axis_size("tm")
    pairs = []
    for block in range(block_count):
        for rank in range(rank_count):
            to = ((block + blocks) % block_count) * rank_count + (rank + ranks) % rank_count
            pairs.append((block * rank_count + rank, to))
    return lax.ppermute(value, ("chan", "tm"), pairs)


def swapped(value):
    return lax.ppermute(value, "chan", [(block, block ^ 1) for block in range(lax.axis_size("chan"))])


def shards(traces, plan, dead_channels):
    windows, channels, _ = traces.shape
    ranks = lax.axis_size("tm")
    share = channels // ranks
    assert ranks % 2 == 0 and share % min(STEP, share) == 0
    first_channel = (lax.axis_index("chan") * channels).astype(jnp.int32).reshape(1)
    rank = lax.axis_index("tm").astype(jnp.int32).reshape(1)
    mine, weights, lags = block_spectra(traces, dead_channels, plan, first_channel, windows * ranks)
    behind = [moved(mine, 2, step) for step in reversed(range(ranks))][::-1]
    own = [mine] + [moved(mine, 0, step) for step in range(1, ranks)]
    run = functools.partial(
        correlate, rank=rank, weights=weights, lags=lags, own=own, share=share
    )
    result = run((0,), far=own)
    behind, result = lax.optimization_barrier((behind, result))
    odd = lax.axis_index("chan") % 2 == 1
    beside = [swapped(jnp.where(odd, far, near)) for far, near in zip(behind, own, strict=True)]
    if MERGED:
        return run((1, 2), far=beside + behind, previous=result)
    result = run((2,), far=behind, previous=result)
    return run((1,), far=beside, previous=result)


def solution(mesh):
    in_specs = (P("tm", "chan", None), P("chan", None), P())
    out_specs = P("chan", "tm", None, None, None)
    return jax.shard_map(shards, mesh=mesh, in_specs=in_specs, out_specs=out_specs, check_vma=False)
```

```python
import functools
import math

import jax
import jax.numpy as jnp
import ml_dtypes
import numpy as np
from jax import lax
from jax.experimental import pallas as pl
from jax.experimental.pallas import tpu as pltpu
from jax.sharding import PartitionSpec as P

BINS = 128
HALF_LAG = 64
OFFS = 3
LAGS = 2 * HALF_LAG + 1
WATER_LEVEL = 0.1
EPSILON = 1e-06

LANES = 128
RUN = 16
GROUPS = BINS // RUN
STEP = 16
BATCH = 4
SEGMENT = 256
VMEM_LIMIT = 24 << 20
MERGED = True

F32 = jnp.float32
BF16 = jnp.bfloat16


def dft_tables(samples):
    bins = np.arange(1, BINS + 1)[None, :]
    phase = np.arange(SEGMENT)[:, None] * bins % samples * (2.0 * math.pi / samples)
    table = np.concatenate([np.cos(phase), -np.sin(phase)], axis=1)
    high = table.astype(ml_dtypes.bfloat16)
    low = (table - high.astype(np.float64)).astype(ml_dtypes.bfloat16)
    starts = np.arange(0, samples, SEGMENT)[:, None]
    turn = starts * bins % samples * (2.0 * math.pi / samples)
    turns = np.concatenate([np.cos(turn), -np.sin(turn)], axis=1).astype(np.float32)
    return high, low, turns


def lag_table(samples, total_windows):
    lags = np.arange(-HALF_LAG, HALF_LAG + 1)
    phase = (np.arange(1, BINS + 1)[:, None] * lags[None, :]) % samples
    phase = phase * (2.0 * math.pi / samples)
    table = np.concatenate([np.cos(phase), -np.sin(phase)], axis=0)
    return (table / math.sqrt(BINS * total_windows)).astype(ml_dtypes.bfloat16)


def spectra_kernel(first_ref, *refs):
    hbm, (out_ref, weight_ref, lag_ref), places, (tail_ref, sems) = refs[:7], refs[7:10], refs[10:16], refs[16:]
    places = (*places, lag_ref)
    trace_hbm, held_ref = hbm[0], places[0]
    dead_ref, plan_ref, high_ref, low_ref, turn_ref = places[1:6]
    windows, channels, samples = trace_hbm.shape

    def copy(window):
        return pltpu.make_async_copy(trace_hbm.at[window], held_ref.at[window], sems.at[window])

    small = [
        pltpu.make_async_copy(source, place, sems.at[windows + index])
        for index, (source, place) in enumerate(zip(hbm[1:], places[1:], strict=True))
    ]
    for one in (small[2], small[3]):
        one.start()
    for window in range(windows):
        copy(window).start()
    for one in (*small[:2], *small[4:]):
        one.start()
    dot = functools.partial(jnp.dot, preferred_element_type=F32)
    segments = pl.cdiv(samples, SEGMENT)
    last = samples - (segments - 1) * SEGMENT
    tail_ref[...] = jnp.zeros_like(tail_ref)
    small[2].wait()
    small[3].wait()
    high_table, low_table = high_ref[...], low_ref[...]
    def transformed(window):
        tail_ref[window % 2, :, :last] = held_ref[window, :, samples - last : samples]
        highs, lows = [], []
        for segment in range(segments):
            if segment == segments - 1:
                piece = tail_ref[window % 2]
            else:
                piece = held_ref[window, :, segment * SEGMENT : (segment + 1) * SEGMENT]
            highs.append(piece.astype(BF16))
            lows.append((piece - highs[-1].astype(F32)).astype(BF16))
        high = jnp.concatenate(highs, axis=0)
        low = jnp.concatenate(lows, axis=0)
        return dot(high, high_table) + dot(low, high_table) + dot(high, low_table)

    def whitened(all_raw):
        real = imag = None
        for segment in range(segments):
            raw = all_raw[segment * channels : (segment + 1) * channels]
            if segment == 0:
                real, imag = raw[:, :BINS], raw[:, BINS:]
            else:
                cosine = turn_ref[segment : segment + 1, :BINS]
                sine = turn_ref[segment : segment + 1, BINS:]
                real += raw[:, :BINS] * cosine - raw[:, BINS:] * sine
                imag += raw[:, BINS:] * cosine + raw[:, :BINS] * sine
        power = real * real + imag * imag
        mean = jnp.sum(power, axis=1, keepdims=True) * (1.0 / BINS)
        factor = lax.rsqrt(power + WATER_LEVEL * mean + EPSILON) * live
        return real * factor, imag * factor

    pairs = []
    live = all_raw = None
    for window in range(windows):
        if window % 2 == 0:
            copy(window).wait()
            copy(window + 1).wait()
        if window == 1:
            for one in (*small[:2], *small[4:]):
                one.wait()
        now = transformed(window)
        if window == 1:
            ids = first_ref[0] + lax.broadcasted_iota(jnp.int32, (channels, 1), 0)
            dead = jnp.where(ids == dead_ref[...], 1.0, 0.0)
            live = 1.0 - jnp.max(dead, axis=1, keepdims=True)
            weight_ref[...] = jnp.zeros_like(weight_ref)
            for offset in range(OFFS):
                weight = plan_ref[:, offset : offset + 1].astype(F32)
                weight_ref[offset : offset + 1, :] = jnp.broadcast_to(weight, (1, LANES))
        if window > 0:
            pairs.append(whitened(all_raw))
        all_raw = now
    pairs.append(whitened(all_raw))
    reals, imags = [pair[0] for pair in pairs], [pair[1] for pair in pairs]
    parts = reals + imags
    run_of = lax.broadcasted_iota(jnp.int32, (1, LANES), 1) // RUN
    for bit in (1, 2, 4):
        keep = (run_of & bit) == 0
        for index in range(len(parts)):
            if index & bit:
                continue
            first, second = parts[index], parts[index | bit]
            parts[index] = jnp.where(keep, first, pltpu.roll(second, bit * RUN, 1))
            parts[index | bit] = jnp.where(keep, pltpu.roll(first, LANES - bit * RUN, 1), second)
    for group, part in enumerate(parts):
        out_ref[:, group * LANES : (group + 1) * LANES] = part.astype(BF16)


def block_spectra(traces, dead_channels, plan, first_channel, total_windows):
    windows, channels, samples = traces.shape
    assert 2 * windows == LANES // RUN and GROUPS == 2 * windows
    high, low, turns = (jnp.asarray(table) for table in dft_tables(samples))
    lags = jnp.asarray(lag_table(samples, total_windows))
    arrays = [traces, dead_channels[None, :], plan, high, low, turns, lags]
    arrays = [pltpu.with_memory_space_constraint(array, pltpu.HBM) for array in arrays]
    vmem = pl.BlockSpec(memory_space=pltpu.VMEM)
    return pl.pallas_call(
        spectra_kernel,
        out_shape=[
            jax.ShapeDtypeStruct((channels, GROUPS * LANES), BF16),
            jax.ShapeDtypeStruct((8, LANES), F32),
            jax.ShapeDtypeStruct(lags.shape, lags.dtype),
        ],
        in_specs=[pl.BlockSpec(memory_space=pltpu.SMEM)]
        + [pl.BlockSpec(memory_space=pltpu.HBM)] * len(arrays),
        out_specs=[vmem] * 3,
        scratch_shapes=[pltpu.VMEM(array.shape, array.dtype) for array in arrays[:-1]]
        + [
            pltpu.VMEM((2, channels, SEGMENT), F32),
            pltpu.SemaphoreType.DMA((windows + len(arrays) - 1,)),
        ],
        compiler_params=pltpu.CompilerParams(vmem_limit_bytes=VMEM_LIMIT),
        name="spectra",
    )(first_channel, *arrays)


def correlation_kernel(offsets, sources, share, step_rows, rank_ref, weight_ref, lag_ref, *refs):
    own_refs, refs = refs[:sources], refs[sources:]
    far_refs, refs = refs[: sources * len(offsets)], refs[sources * len(offsets) :]
    out_ref, near_ref, far_ref, cross_ref, lagged_ref, sems = refs[-6:]
    channels = own_refs[0].shape[0]
    columns = len(offsets) * channels
    pairs = sources // 2
    first_row = rank_ref[0] * share

    def lanes_of(source, group):
        start = ((source // 2) * GROUPS + group) * 2 * LANES + (source % 2) * LANES
        return slice(start, start + LANES)

    held_first = first_row
    for source, own_ref in enumerate(own_refs):
        for group in range(GROUPS):
            at = slice(group * LANES, (group + 1) * LANES)
            if share % 16 == 0:
                value = own_ref[pl.ds(pl.multiple_of(first_row, share), share), at]
                held_first = 0
            else:
                value = own_ref[:, at]
            near_ref[:, lanes_of(source, group)] = value.astype(F32)
    sign = jnp.where(lax.broadcasted_iota(jnp.int32, (1, LANES), 1) < LANES // 2, -1.0, 1.0)
    for place, offset in enumerate(offsets):
        weight = weight_ref[offset : offset + 1, :]
        turned_weight = weight * sign
        rows = slice(place * channels, (place + 1) * channels)
        turned_rows = slice(columns + place * channels, columns + (place + 1) * channels)
        for source in range(sources):
            far = far_refs[place * sources + source]
            lanes = slice((source % 2) * LANES, (source % 2 + 1) * LANES)
            for group in range(GROUPS):
                value = far[:, group * LANES : (group + 1) * LANES].astype(F32)
                turned = pltpu.roll(value, LANES // 2, 1) * turned_weight
                slot = (source // 2) * GROUPS + group
                far_ref[slot, rows, lanes] = (value * weight).astype(BF16)
                far_ref[slot, turned_rows, lanes] = turned.astype(BF16)

    diagonal = (
        lax.broadcasted_iota(jnp.int32, (RUN, 2 * LANES), 1) % RUN
        == lax.broadcasted_iota(jnp.int32, (RUN, 2 * LANES), 0)
    )
    column = lax.broadcasted_iota(jnp.int32, (1, 2 * columns), 1) % channels
    lags = lag_ref[...]

    batch = min(BATCH, step_rows)

    def copy(index):
        return pltpu.make_async_copy(
            lagged_ref.at[index],
            out_ref.at[0, pl.ds(index * batch, batch), pl.ds(offsets[0], len(offsets))],
            sems.at[index],
        )

    def one_step(step, carry):
        for group in range(GROUPS):
            total = None
            for pair in range(pairs):
                blocks = []
                slot = pair * GROUPS + group
                lanes = slice(slot * 2 * LANES, (slot + 1) * 2 * LANES)
                for row in range(step_rows):
                    one = near_ref[pl.ds(held_first + step * step_rows + row, 1), lanes]
                    spread = jnp.broadcast_to(one, (RUN, 2 * LANES))
                    blocks.append(jnp.where(diagonal, spread, 0.0).astype(BF16))
                term = lax.dot_general(
                    jnp.concatenate(blocks, axis=0),
                    far_ref[slot],
                    (((1,), (1,)), ((), ())),
                    preferred_element_type=F32,
                )
                total = term if total is None else total + term
            for row in range(step_rows):
                value = total[row * RUN : (row + 1) * RUN]
                if offsets[0] == 0:
                    value = jnp.where(column > first_row + step * step_rows + row, value, 0.0)
                cross_ref[row, group * RUN : (group + 1) * RUN, :] = value.astype(BF16)
        for start in range(0, step_rows, batch):
            sides = []
            for row in range(start, start + batch):
                cross = cross_ref[row].T
                sides.append(jnp.concatenate([cross[:columns], cross[columns:]], axis=1))
            lagged = jnp.dot(jnp.concatenate(sides, axis=0), lags, preferred_element_type=F32)
            index = (step * step_rows + start) // batch
            lagged_ref[index] = lagged.reshape(batch, len(offsets), channels, LAGS)
            copy(index).start()
        return carry

    lax.fori_loop(0, share // step_rows, one_step, 0, unroll=True)
    for index in range(share // batch):
        copy(index).wait()


def correlate(offsets, rank, weights, lags, own, far, share, previous=None):
    sources = len(own)
    channels = own[0].shape[0]
    count = len(offsets)
    pairs = sources // 2
    vmem = pl.BlockSpec(memory_space=pltpu.VMEM)
    smem = pl.BlockSpec(memory_space=pltpu.SMEM)
    hbm = pl.BlockSpec(memory_space=pltpu.HBM)
    arrays = [rank, weights, lags, *own, *far]
    in_specs = [smem] + [vmem] * (len(arrays) - 1)
    aliases = {}
    if previous is not None:
        aliases = {len(arrays): 0}
        arrays.append(previous)
        in_specs.append(hbm)
    step_rows = min(STEP, share)
    batch = min(BATCH, step_rows)
    held = share if share % 16 == 0 else channels
    return pl.pallas_call(
        functools.partial(correlation_kernel, offsets, sources, share, step_rows),
        out_shape=jax.ShapeDtypeStruct((1, share, OFFS, channels, LAGS), F32),
        in_specs=in_specs,
        out_specs=hbm,
        scratch_shapes=[
            pltpu.VMEM((held, pairs * GROUPS * 2 * LANES), F32),
            pltpu.VMEM((pairs * GROUPS, 2 * count * channels, 2 * LANES), BF16),
            pltpu.VMEM((step_rows, BINS, 2 * count * channels), BF16),
            pltpu.VMEM((share // batch, batch, count, channels, LAGS), F32),
            pltpu.SemaphoreType.DMA((share // batch,)),
        ],
        compiler_params=pltpu.CompilerParams(vmem_limit_bytes=VMEM_LIMIT),
        input_output_aliases=aliases,
        cost_estimate=pl.CostEstimate(
            flops=2 * share * 2 * BINS * 2 * LANES * pairs * channels * count,
            bytes_accessed=share * count * channels * 2 * LANES * 4,
            transcendentals=0,
        ),
        name="correlate_" + "_".join(str(offset) for offset in offsets),
    )(*arrays)


def moved(value, blocks, ranks):
    block_count, rank_count = lax.axis_size("chan"), lax.axis_size("tm")
    pairs = []
    for block in range(block_count):
        for rank in range(rank_count):
            to = ((block + blocks) % block_count) * rank_count + (rank + ranks) % rank_count
            pairs.append((block * rank_count + rank, to))
    return lax.ppermute(value, ("chan", "tm"), pairs)


def held(value):
    vmem = pl.BlockSpec(memory_space=pltpu.VMEM)

    def body(in_ref, out_ref):
        out_ref[...] = in_ref[...]

    return pl.pallas_call(
        body,
        out_shape=jax.ShapeDtypeStruct(value.shape, value.dtype),
        in_specs=[vmem],
        out_specs=vmem,
        compiler_params=pltpu.CompilerParams(vmem_limit_bytes=VMEM_LIMIT),
        cost_estimate=pl.CostEstimate(flops=10**10, bytes_accessed=10**8, transcendentals=0),
        name="held",
    )(value)


def swapped(value):
    return lax.ppermute(value, "chan", [(block, block ^ 1) for block in range(lax.axis_size("chan"))])


def shards(traces, plan, dead_channels):
    windows, channels, _ = traces.shape
    ranks = lax.axis_size("tm")
    share = channels // ranks
    assert ranks % 2 == 0 and share % min(STEP, share) == 0
    first_channel = (lax.axis_index("chan") * channels).astype(jnp.int32).reshape(1)
    rank = lax.axis_index("tm").astype(jnp.int32).reshape(1)
    mine, weights, lags = block_spectra(traces, dead_channels, plan, first_channel, windows * ranks)
    behind = [moved(mine, 2, step) for step in reversed(range(ranks))][::-1]
    own = [mine] + [moved(mine, 0, step) for step in range(1, ranks)]
    weights = held(weights)
    run = functools.partial(
        correlate, rank=rank, weights=weights, lags=lags, own=own, share=share
    )
    result = run((0,), far=own)
    behind, result = lax.optimization_barrier((behind, result))
    odd = lax.axis_index("chan") % 2 == 1
    beside = [swapped(jnp.where(odd, far, near)) for far, near in zip(behind, own, strict=True)]
    if MERGED:
        return run((1, 2), far=beside + behind, previous=result)
    result = run((2,), far=behind, previous=result)
    return run((1,), far=beside, previous=result)


def solution(mesh):
    in_specs = (P("tm", "chan", None), P("chan", None), P())
    out_specs = P("chan", "tm", None, None, None)
    return jax.shard_map(shards, mesh=mesh, in_specs=in_specs, out_specs=out_specs, check_vma=False)
```

```python
import functools
import math

import jax
import jax.numpy as jnp
import ml_dtypes
import numpy as np
from jax import lax
from jax.experimental import pallas as pl
from jax.experimental.pallas import tpu as pltpu
from jax.sharding import PartitionSpec as P

BINS = 128
HALF_LAG = 64
OFFS = 3
LAGS = 2 * HALF_LAG + 1
WATER_LEVEL = 0.1
EPSILON = 1e-06

LANES = 128
RUN = 16
GROUPS = BINS // RUN
BATCH = 4
SEGMENT = 256
VMEM_LIMIT = 24 << 20
STEPS = (16, 16)

F32 = jnp.float32
BF16 = jnp.bfloat16


def dft_tables(samples):
    bins = np.arange(1, BINS + 1)[None, :]
    phase = np.arange(SEGMENT)[:, None] * bins % samples * (2.0 * math.pi / samples)
    table = np.concatenate([np.cos(phase), -np.sin(phase)], axis=1)
    high = table.astype(ml_dtypes.bfloat16)
    low = (table - high.astype(np.float64)).astype(ml_dtypes.bfloat16)
    starts = np.arange(0, samples, SEGMENT)[:, None]
    turn = starts * bins % samples * (2.0 * math.pi / samples)
    turns = np.concatenate([np.cos(turn), -np.sin(turn)], axis=1).astype(np.float32)
    return high, low, turns


def lag_table(samples, total_windows):
    lags = np.arange(-HALF_LAG, HALF_LAG + 1)
    phase = (np.arange(1, BINS + 1)[:, None] * lags[None, :]) % samples
    phase = phase * (2.0 * math.pi / samples)
    table = np.concatenate([np.cos(phase), -np.sin(phase)], axis=0)
    return (table / math.sqrt(BINS * total_windows)).astype(ml_dtypes.bfloat16)


def spectra_kernel(first_ref, *refs):
    hbm, (out_ref, weight_ref, lag_ref), places, (tail_ref, sems) = refs[:7], refs[7:10], refs[10:16], refs[16:]
    places = (*places, lag_ref)
    trace_hbm, held_ref = hbm[0], places[0]
    dead_ref, plan_ref, high_ref, low_ref, turn_ref = places[1:6]
    windows, channels, samples = trace_hbm.shape

    def copy(window):
        return pltpu.make_async_copy(trace_hbm.at[window], held_ref.at[window], sems.at[window])

    small = [
        pltpu.make_async_copy(source, place, sems.at[windows + index])
        for index, (source, place) in enumerate(zip(hbm[1:], places[1:], strict=True))
    ]
    for one in (small[2], small[3]):
        one.start()
    for window in range(windows):
        copy(window).start()
    for one in (*small[:2], *small[4:]):
        one.start()
    dot = functools.partial(jnp.dot, preferred_element_type=F32)
    segments = pl.cdiv(samples, SEGMENT)
    last = samples - (segments - 1) * SEGMENT
    tail_ref[...] = jnp.zeros_like(tail_ref)
    small[2].wait()
    small[3].wait()
    high_table, low_table = high_ref[...], low_ref[...]
    def transformed(window):
        tail_ref[window % 2, :, :last] = held_ref[window, :, samples - last : samples]
        highs, lows = [], []
        for segment in range(segments):
            if segment == segments - 1:
                piece = tail_ref[window % 2]
            else:
                piece = held_ref[window, :, segment * SEGMENT : (segment + 1) * SEGMENT]
            highs.append(piece.astype(BF16))
            lows.append((piece - highs[-1].astype(F32)).astype(BF16))
        high = jnp.concatenate(highs, axis=0)
        low = jnp.concatenate(lows, axis=0)
        return dot(high, high_table) + dot(low, high_table) + dot(high, low_table)

    def whitened(all_raw):
        real = imag = None
        for segment in range(segments):
            raw = all_raw[segment * channels : (segment + 1) * channels]
            if segment == 0:
                real, imag = raw[:, :BINS], raw[:, BINS:]
            else:
                cosine = turn_ref[segment : segment + 1, :BINS]
                sine = turn_ref[segment : segment + 1, BINS:]
                real += raw[:, :BINS] * cosine - raw[:, BINS:] * sine
                imag += raw[:, BINS:] * cosine + raw[:, :BINS] * sine
        power = real * real + imag * imag
        mean = jnp.sum(power, axis=1, keepdims=True) * (1.0 / BINS)
        factor = lax.rsqrt(power + WATER_LEVEL * mean + EPSILON) * live
        return real * factor, imag * factor

    pairs = []
    live = all_raw = None
    for window in range(windows):
        if window % 2 == 0:
            copy(window).wait()
            copy(window + 1).wait()
        if window == 1:
            for one in (*small[:2], *small[4:]):
                one.wait()
        now = transformed(window)
        if window == 1:
            ids = first_ref[0] + lax.broadcasted_iota(jnp.int32, (channels, 1), 0)
            dead = jnp.where(ids == dead_ref[...], 1.0, 0.0)
            live = 1.0 - jnp.max(dead, axis=1, keepdims=True)
            weight_ref[...] = jnp.zeros_like(weight_ref)
            for offset in range(OFFS):
                weight = plan_ref[:, offset : offset + 1].astype(F32)
                weight_ref[offset : offset + 1, :] = jnp.broadcast_to(weight, (1, LANES))
        if window > 0:
            pairs.append(whitened(all_raw))
        all_raw = now
    pairs.append(whitened(all_raw))
    reals, imags = [pair[0] for pair in pairs], [pair[1] for pair in pairs]
    parts = reals + imags
    run_of = lax.broadcasted_iota(jnp.int32, (1, LANES), 1) // RUN
    for bit in (1, 2, 4):
        keep = (run_of & bit) == 0
        for index in range(len(parts)):
            if index & bit:
                continue
            first, second = parts[index], parts[index | bit]
            parts[index] = jnp.where(keep, first, pltpu.roll(second, bit * RUN, 1))
            parts[index | bit] = jnp.where(keep, pltpu.roll(first, LANES - bit * RUN, 1), second)
    for group, part in enumerate(parts):
        out_ref[:, group * LANES : (group + 1) * LANES] = part.astype(BF16)


def block_spectra(traces, dead_channels, plan, first_channel, total_windows):
    windows, channels, samples = traces.shape
    assert 2 * windows == LANES // RUN and GROUPS == 2 * windows
    high, low, turns = (jnp.asarray(table) for table in dft_tables(samples))
    lags = jnp.asarray(lag_table(samples, total_windows))
    arrays = [traces, dead_channels[None, :], plan, high, low, turns, lags]
    arrays = [pltpu.with_memory_space_constraint(array, pltpu.HBM) for array in arrays]
    vmem = pl.BlockSpec(memory_space=pltpu.VMEM)
    return pl.pallas_call(
        spectra_kernel,
        out_shape=[
            jax.ShapeDtypeStruct((channels, GROUPS * LANES), BF16),
            jax.ShapeDtypeStruct((8, LANES), F32),
            jax.ShapeDtypeStruct(lags.shape, lags.dtype),
        ],
        in_specs=[pl.BlockSpec(memory_space=pltpu.SMEM)]
        + [pl.BlockSpec(memory_space=pltpu.HBM)] * len(arrays),
        out_specs=[vmem] * 3,
        scratch_shapes=[pltpu.VMEM(array.shape, array.dtype) for array in arrays[:-1]]
        + [
            pltpu.VMEM((2, channels, SEGMENT), F32),
            pltpu.SemaphoreType.DMA((windows + len(arrays) - 1,)),
        ],
        compiler_params=pltpu.CompilerParams(vmem_limit_bytes=VMEM_LIMIT),
        name="spectra",
    )(first_channel, *arrays)


def row_steps(share):
    return STEPS if sum(STEPS) == share else (share,)


def correlation_kernel(offset, earlier, last, sources, share, rank_ref, weight_ref, lag_ref, *refs):
    own_refs, far_refs, refs = refs[:sources], refs[sources : 2 * sources], refs[2 * sources :]
    earlier_ref = out_ref = None
    if earlier is not None:
        earlier_ref, refs = refs[0], refs[1:]
    near_ref, far_ref, cross_ref = refs[-4:-1] if not last else refs[-5:-2]
    sems = refs[-1]
    kept_ref = refs[-2] if last else refs[-5]
    if last:
        out_ref = refs[-6]
    elif earlier is not None:
        out_ref = refs[-6]
    channels = own_refs[0].shape[0]
    pairs = sources // 2
    first_row = rank_ref[0] * share
    batch = min(BATCH, share)
    batches = share // batch

    def write_earlier():
        return pltpu.make_async_copy(earlier_ref, out_ref.at[0, :, earlier], sems.at[batches])

    def write(index):
        rows = pl.ds(index * batch, batch)
        return pltpu.make_async_copy(kept_ref.at[rows], out_ref.at[0, rows, offset], sems.at[index])

    if earlier is not None:
        write_earlier().start()

    def lanes_of(source, group):
        start = ((source // 2) * GROUPS + group) * 2 * LANES + (source % 2) * LANES
        return slice(start, start + LANES)

    held_first = first_row
    for source, own_ref in enumerate(own_refs):
        for group in range(GROUPS):
            at = slice(group * LANES, (group + 1) * LANES)
            if share % 16 == 0:
                value = own_ref[pl.ds(pl.multiple_of(first_row, share), share), at]
                held_first = 0
            else:
                value = own_ref[:, at]
            near_ref[:, lanes_of(source, group)] = value.astype(F32)
    sign = jnp.where(lax.broadcasted_iota(jnp.int32, (1, LANES), 1) < LANES // 2, -1.0, 1.0)
    weight = weight_ref[offset : offset + 1, :]
    turned_weight = weight * sign
    for source, far in enumerate(far_refs):
        lanes = slice((source % 2) * LANES, (source % 2 + 1) * LANES)
        for group in range(GROUPS):
            value = far[:, group * LANES : (group + 1) * LANES].astype(F32)
            turned = pltpu.roll(value, LANES // 2, 1) * turned_weight
            slot = (source // 2) * GROUPS + group
            far_ref[slot, :channels, lanes] = (value * weight).astype(BF16)
            far_ref[slot, channels:, lanes] = turned.astype(BF16)

    diagonal = (
        lax.broadcasted_iota(jnp.int32, (RUN, 2 * LANES), 1) % RUN
        == lax.broadcasted_iota(jnp.int32, (RUN, 2 * LANES), 0)
    )
    column = lax.broadcasted_iota(jnp.int32, (1, 2 * channels), 1) % channels
    lags = lag_ref[...]

    def cross_products(first, end):
        for group in range(GROUPS):
            total = None
            for pair in range(pairs):
                blocks = []
                slot = pair * GROUPS + group
                lanes = slice(slot * 2 * LANES, (slot + 1) * 2 * LANES)
                for row in range(first, end):
                    one = near_ref[pl.ds(held_first + row, 1), lanes]
                    spread = jnp.broadcast_to(one, (RUN, 2 * LANES))
                    blocks.append(jnp.where(diagonal, spread, 0.0).astype(BF16))
                term = lax.dot_general(
                    jnp.concatenate(blocks, axis=0),
                    far_ref[slot],
                    (((1,), (1,)), ((), ())),
                    preferred_element_type=F32,
                )
                total = term if total is None else total + term
            for row in range(first, end):
                value = total[(row - first) * RUN : (row - first + 1) * RUN]
                if offset == 0:
                    value = jnp.where(column > first_row + row, value, 0.0)
                cross_ref[row, group * RUN : (group + 1) * RUN, :] = value.astype(BF16)

    def lag_sums(first, end):
        for start in range(first, end, batch):
            sides = []
            for row in range(start, start + batch):
                cross = cross_ref[row].T
                sides.append(jnp.concatenate([cross[:channels], cross[channels:]], axis=1))
            lagged = jnp.dot(jnp.concatenate(sides, axis=0), lags, preferred_element_type=F32)
            kept_ref[start : start + batch] = lagged.reshape(batch, channels, LAGS)
            if last:
                write(start // batch).start()

    first = 0
    for rows in row_steps(share):
        cross_products(first, first + rows)
        lag_sums(first, first + rows)
        first += rows
    if last:
        for index in range(batches):
            write(index).wait()
    if earlier is not None:
        write_earlier().wait()


def correlate(offset, rank, weights, lags, own, far, share, kept=None, earlier=None, previous=None, last=False):
    sources = len(own)
    channels = own[0].shape[0]
    pairs = sources // 2
    vmem = pl.BlockSpec(memory_space=pltpu.VMEM)
    arrays = [rank, weights, lags, *own, *far]
    in_specs = [pl.BlockSpec(memory_space=pltpu.SMEM)] + [vmem] * (len(arrays) - 1)
    out_shape, out_specs, aliases = [], [], {}
    if kept is not None:
        arrays.append(kept)
        in_specs.append(vmem)
        out_shape.append(jax.ShapeDtypeStruct((1, share, OFFS, channels, LAGS), F32))
        out_specs.append(pl.BlockSpec(memory_space=pltpu.HBM))
    if previous is not None:
        aliases = {len(arrays): 0}
        arrays.append(previous)
        in_specs.append(pl.BlockSpec(memory_space=pltpu.HBM))
    lagged = (share, channels, LAGS)
    if not last:
        out_shape.append(jax.ShapeDtypeStruct(lagged, F32))
        out_specs.append(vmem)
    batch = min(BATCH, share)
    assert all(rows % batch == 0 for rows in row_steps(share))
    held = share if share % 16 == 0 else channels
    return pl.pallas_call(
        functools.partial(correlation_kernel, offset, earlier, last, sources, share),
        out_shape=out_shape,
        in_specs=in_specs,
        out_specs=out_specs,
        scratch_shapes=[
            pltpu.VMEM((held, pairs * GROUPS * 2 * LANES), F32),
            pltpu.VMEM((pairs * GROUPS, 2 * channels, 2 * LANES), BF16),
            pltpu.VMEM((share, BINS, 2 * channels), BF16),
        ]
        + ([pltpu.VMEM(lagged, F32)] if last else [])
        + [pltpu.SemaphoreType.DMA((share // batch + 1,))],
        compiler_params=pltpu.CompilerParams(vmem_limit_bytes=VMEM_LIMIT),
        input_output_aliases=aliases,
        cost_estimate=pl.CostEstimate(
            flops=2 * share * 2 * BINS * 2 * LANES * pairs * channels,
            bytes_accessed=share * channels * 2 * LANES * 4,
            transcendentals=0,
        ),
        name=f"correlate_{offset}",
    )(*arrays)


def exchanges(ranks):
    return [(2, step) for step in range(ranks)] + [(0, step) for step in range(1, ranks)]


def moved(value, blocks, ranks):
    block_count, rank_count = lax.axis_size("chan"), lax.axis_size("tm")
    pairs = []
    for block in range(block_count):
        for rank in range(rank_count):
            to = ((block + blocks) % block_count) * rank_count + (rank + ranks) % rank_count
            pairs.append((block * rank_count + rank, to))
    return lax.ppermute(value, ("chan", "tm"), pairs)


def swapped(value):
    return lax.ppermute(value, "chan", [(block, block ^ 1) for block in range(lax.axis_size("chan"))])


def shards(traces, plan, dead_channels):
    windows, channels, _ = traces.shape
    ranks = lax.axis_size("tm")
    share = channels // ranks
    assert ranks % 2 == 0
    first_channel = (lax.axis_index("chan") * channels).astype(jnp.int32).reshape(1)
    rank = lax.axis_index("tm").astype(jnp.int32).reshape(1)
    mine, weights, lags = block_spectra(traces, dead_channels, plan, first_channel, windows * ranks)
    received = {}
    for blocks, step in exchanges(ranks):
        received[blocks, step] = moved(mine, blocks, step)
    behind = [received[2, step] for step in range(ranks)]
    own = [mine] + [received[0, step] for step in range(1, ranks)]
    odd = lax.axis_index("chan") % 2 == 1
    run = functools.partial(correlate, rank=rank, weights=weights, lags=lags, own=own, share=share)
    beside = [swapped(jnp.where(odd, behind[0], mine))]
    (kept,) = run(0, far=own)
    later, kept = lax.optimization_barrier((behind[1:], kept))
    behind = behind[:1] + later
    beside += [swapped(jnp.where(odd, far, near)) for far, near in zip(behind[1:], own[1:], strict=True)]
    result, kept = run(2, far=behind, kept=kept, earlier=0)
    (result,) = run(1, far=beside, kept=kept, earlier=2, previous=result, last=True)
    return result


def solution(mesh):
    in_specs = (P("tm", "chan", None), P("chan", None), P())
    out_specs = P("chan", "tm", None, None, None)
    return jax.shard_map(shards, mesh=mesh, in_specs=in_specs, out_specs=out_specs, check_vma=False)
```

```python
import functools
import math

import jax
import jax.numpy as jnp
import ml_dtypes
import numpy as np
from jax import lax
from jax.experimental import pallas as pl
from jax.experimental.pallas import tpu as pltpu
from jax.sharding import PartitionSpec as P

BINS = 128
HALF_LAG = 64
OFFS = 3
LAGS = 2 * HALF_LAG + 1
WATER_LEVEL = 0.1
EPSILON = 1e-06

LANES = 128
RUN = 16
GROUPS = BINS // RUN
BATCH = 4
SEGMENT = 256
VMEM_LIMIT = 24 << 20
STEPS = (16, 16)

F32 = jnp.float32
BF16 = jnp.bfloat16


def dft_tables(samples):
    bins = np.arange(1, BINS + 1)[None, :]
    phase = np.arange(SEGMENT)[:, None] * bins % samples * (2.0 * math.pi / samples)
    table = np.concatenate([np.cos(phase), -np.sin(phase)], axis=1)
    high = table.astype(ml_dtypes.bfloat16)
    low = (table - high.astype(np.float64)).astype(ml_dtypes.bfloat16)
    starts = np.arange(0, samples, SEGMENT)[:, None]
    turn = starts * bins % samples * (2.0 * math.pi / samples)
    turns = np.concatenate([np.cos(turn), -np.sin(turn)], axis=1).astype(np.float32)
    return high, low, turns


def lag_table(samples, total_windows):
    lags = np.arange(-HALF_LAG, HALF_LAG + 1)
    phase = (np.arange(1, BINS + 1)[:, None] * lags[None, :]) % samples
    phase = phase * (2.0 * math.pi / samples)
    table = np.concatenate([np.cos(phase), -np.sin(phase)], axis=0)
    return (table / math.sqrt(BINS * total_windows)).astype(ml_dtypes.bfloat16)


def spectra_kernel(first_ref, *refs):
    hbm, (out_ref, weight_ref, lag_ref), places, (tail_ref, sems) = refs[:7], refs[7:10], refs[10:16], refs[16:]
    places = (*places, lag_ref)
    trace_hbm, held_ref = hbm[0], places[0]
    dead_ref, plan_ref, high_ref, low_ref, turn_ref = places[1:6]
    windows, channels, samples = trace_hbm.shape

    def copy(window):
        return pltpu.make_async_copy(trace_hbm.at[window], held_ref.at[window], sems.at[window])

    small = [
        pltpu.make_async_copy(source, place, sems.at[windows + index])
        for index, (source, place) in enumerate(zip(hbm[1:], places[1:], strict=True))
    ]
    for one in (small[2], small[3]):
        one.start()
    for window in range(windows):
        copy(window).start()
    for one in (*small[:2], *small[4:]):
        one.start()
    dot = functools.partial(jnp.dot, preferred_element_type=F32)
    segments = pl.cdiv(samples, SEGMENT)
    last = samples - (segments - 1) * SEGMENT
    tail_ref[...] = jnp.zeros_like(tail_ref)
    small[2].wait()
    small[3].wait()
    high_table, low_table = high_ref[...], low_ref[...]
    def transformed():
        highs, lows = [], []
        for segment in range(segments):
            for window in range(windows):
                if segment == segments - 1:
                    tail_ref[window, :, :last] = held_ref[window, :, samples - last : samples]
                    piece = tail_ref[window]
                else:
                    piece = held_ref[window, :, segment * SEGMENT : (segment + 1) * SEGMENT]
                highs.append(piece.astype(BF16))
                lows.append((piece - highs[-1].astype(F32)).astype(BF16))
        high = jnp.concatenate(highs, axis=0)
        low = jnp.concatenate(lows, axis=0)
        return dot(high, high_table) + dot(low, high_table) + dot(high, low_table)

    def whitened(all_raw, window):
        real = imag = None
        for segment in range(segments):
            start = (segment * windows + window) * channels
            raw = all_raw[start : start + channels]
            if segment == 0:
                real, imag = raw[:, :BINS], raw[:, BINS:]
            else:
                cosine = turn_ref[segment : segment + 1, :BINS]
                sine = turn_ref[segment : segment + 1, BINS:]
                real += raw[:, :BINS] * cosine - raw[:, BINS:] * sine
                imag += raw[:, BINS:] * cosine + raw[:, :BINS] * sine
        power = real * real + imag * imag
        mean = jnp.sum(power, axis=1, keepdims=True) * (1.0 / BINS)
        factor = lax.rsqrt(power + WATER_LEVEL * mean + EPSILON) * live
        return real * factor, imag * factor

    for window in range(windows):
        copy(window).wait()
    for one in (*small[:2], *small[4:]):
        one.wait()
    all_raw = transformed()
    ids = first_ref[0] + lax.broadcasted_iota(jnp.int32, (channels, 1), 0)
    dead = jnp.where(ids == dead_ref[...], 1.0, 0.0)
    live = 1.0 - jnp.max(dead, axis=1, keepdims=True)
    weight_ref[...] = jnp.zeros_like(weight_ref)
    for offset in range(OFFS):
        weight = plan_ref[:, offset : offset + 1].astype(F32)
        weight_ref[offset : offset + 1, :] = jnp.broadcast_to(weight, (1, LANES))
    pairs = [whitened(all_raw, window) for window in range(windows)]
    reals, imags = [pair[0] for pair in pairs], [pair[1] for pair in pairs]
    parts = reals + imags
    run_of = lax.broadcasted_iota(jnp.int32, (1, LANES), 1) // RUN
    for bit in (4, 1, 2):
        keep = (run_of & bit) == 0
        for index in range(len(parts)):
            if index & bit:
                continue
            first, second = parts[index], parts[index | bit]
            parts[index] = jnp.where(keep, first, pltpu.roll(second, bit * RUN, 1))
            parts[index | bit] = jnp.where(keep, pltpu.roll(first, LANES - bit * RUN, 1), second)
    for group, part in enumerate(parts):
        out_ref[:, group * LANES : (group + 1) * LANES] = part.astype(BF16)


def block_spectra(traces, dead_channels, plan, first_channel, total_windows):
    windows, channels, samples = traces.shape
    assert 2 * windows == LANES // RUN and GROUPS == 2 * windows
    high, low, turns = (jnp.asarray(table) for table in dft_tables(samples))
    lags = jnp.asarray(lag_table(samples, total_windows))
    arrays = [traces, dead_channels[None, :], plan, high, low, turns, lags]
    arrays = [pltpu.with_memory_space_constraint(array, pltpu.HBM) for array in arrays]
    vmem = pl.BlockSpec(memory_space=pltpu.VMEM)
    return pl.pallas_call(
        spectra_kernel,
        out_shape=[
            jax.ShapeDtypeStruct((channels, GROUPS * LANES), BF16),
            jax.ShapeDtypeStruct((8, LANES), F32),
            jax.ShapeDtypeStruct(lags.shape, lags.dtype),
        ],
        in_specs=[pl.BlockSpec(memory_space=pltpu.SMEM)]
        + [pl.BlockSpec(memory_space=pltpu.HBM)] * len(arrays),
        out_specs=[vmem] * 3,
        scratch_shapes=[pltpu.VMEM(array.shape, array.dtype) for array in arrays[:-1]]
        + [
            pltpu.VMEM((windows, channels, SEGMENT), F32),
            pltpu.SemaphoreType.DMA((windows + len(arrays) - 1,)),
        ],
        compiler_params=pltpu.CompilerParams(vmem_limit_bytes=VMEM_LIMIT),
        name="spectra",
    )(first_channel, *arrays)


def row_steps(share):
    return STEPS if sum(STEPS) == share else (share,)


def correlation_kernel(offset, earlier, last, sources, share, rank_ref, weight_ref, lag_ref, *refs):
    own_refs, far_refs, refs = refs[:sources], refs[sources : 2 * sources], refs[2 * sources :]
    earlier_ref = out_ref = None
    if earlier is not None:
        earlier_ref, refs = refs[0], refs[1:]
    near_ref, far_ref, cross_ref = refs[-4:-1] if not last else refs[-5:-2]
    sems = refs[-1]
    kept_ref = refs[-2] if last else refs[-5]
    if last:
        out_ref = refs[-6]
    elif earlier is not None:
        out_ref = refs[-6]
    channels = own_refs[0].shape[0]
    pairs = sources // 2
    first_row = rank_ref[0] * share
    batch = min(BATCH, share)
    batches = share // batch

    def write_earlier():
        return pltpu.make_async_copy(earlier_ref, out_ref.at[0, :, earlier], sems.at[batches])

    def write(index):
        rows = pl.ds(index * batch, batch)
        return pltpu.make_async_copy(kept_ref.at[rows], out_ref.at[0, rows, offset], sems.at[index])

    if earlier is not None:
        write_earlier().start()

    def lanes_of(source, group):
        start = ((source // 2) * GROUPS + group) * 2 * LANES + (source % 2) * LANES
        return slice(start, start + LANES)

    held_first = first_row
    for source, own_ref in enumerate(own_refs):
        for group in range(GROUPS):
            at = slice(group * LANES, (group + 1) * LANES)
            if share % 16 == 0:
                value = own_ref[pl.ds(pl.multiple_of(first_row, share), share), at]
                held_first = 0
            else:
                value = own_ref[:, at]
            near_ref[:, lanes_of(source, group)] = value.astype(F32)
    sign = jnp.where(lax.broadcasted_iota(jnp.int32, (1, LANES), 1) < LANES // 2, -1.0, 1.0)
    weight = weight_ref[offset : offset + 1, :]
    turned_weight = weight * sign
    for source, far in enumerate(far_refs):
        lanes = slice((source % 2) * LANES, (source % 2 + 1) * LANES)
        for group in range(GROUPS):
            value = far[:, group * LANES : (group + 1) * LANES].astype(F32)
            turned = pltpu.roll(value, LANES // 2, 1) * turned_weight
            slot = (source // 2) * GROUPS + group
            far_ref[slot, :channels, lanes] = (value * weight).astype(BF16)
            far_ref[slot, channels:, lanes] = turned.astype(BF16)

    diagonal = (
        lax.broadcasted_iota(jnp.int32, (RUN, 2 * LANES), 1) % RUN
        == lax.broadcasted_iota(jnp.int32, (RUN, 2 * LANES), 0)
    )
    column = lax.broadcasted_iota(jnp.int32, (1, 2 * channels), 1) % channels
    lags = lag_ref[...]

    def cross_products(first, end):
        for group in range(GROUPS):
            total = None
            for pair in range(pairs):
                blocks = []
                slot = pair * GROUPS + group
                lanes = slice(slot * 2 * LANES, (slot + 1) * 2 * LANES)
                for row in range(first, end):
                    one = near_ref[pl.ds(held_first + row, 1), lanes]
                    spread = jnp.broadcast_to(one, (RUN, 2 * LANES))
                    blocks.append(jnp.where(diagonal, spread, 0.0).astype(BF16))
                term = lax.dot_general(
                    jnp.concatenate(blocks, axis=0),
                    far_ref[slot],
                    (((1,), (1,)), ((), ())),
                    preferred_element_type=F32,
                )
                total = term if total is None else total + term
            for row in range(first, end):
                value = total[(row - first) * RUN : (row - first + 1) * RUN]
                if offset == 0:
                    value = jnp.where(column > first_row + row, value, 0.0)
                cross_ref[row, group * RUN : (group + 1) * RUN, :] = value.astype(BF16)

    def lag_sums(first, end):
        for start in range(first, end, batch):
            sides = []
            for row in range(start, start + batch):
                cross = cross_ref[row].T
                sides.append(jnp.concatenate([cross[:channels], cross[channels:]], axis=1))
            lagged = jnp.dot(jnp.concatenate(sides, axis=0), lags, preferred_element_type=F32)
            kept_ref[start : start + batch] = lagged.reshape(batch, channels, LAGS)
            if last:
                write(start // batch).start()

    first = 0
    for rows in row_steps(share):
        cross_products(first, first + rows)
        lag_sums(first, first + rows)
        first += rows
    if last:
        for index in range(batches):
            write(index).wait()
    if earlier is not None:
        write_earlier().wait()


def correlate(offset, rank, weights, lags, own, far, share, kept=None, earlier=None, previous=None, last=False):
    sources = len(own)
    channels = own[0].shape[0]
    pairs = sources // 2
    vmem = pl.BlockSpec(memory_space=pltpu.VMEM)
    arrays = [rank, weights, lags, *own, *far]
    in_specs = [pl.BlockSpec(memory_space=pltpu.SMEM)] + [vmem] * (len(arrays) - 1)
    out_shape, out_specs, aliases = [], [], {}
    if kept is not None:
        arrays.append(kept)
        in_specs.append(vmem)
        out_shape.append(jax.ShapeDtypeStruct((1, share, OFFS, channels, LAGS), F32))
        out_specs.append(pl.BlockSpec(memory_space=pltpu.HBM))
    if previous is not None:
        aliases = {len(arrays): 0}
        arrays.append(previous)
        in_specs.append(pl.BlockSpec(memory_space=pltpu.HBM))
    lagged = (share, channels, LAGS)
    if not last:
        out_shape.append(jax.ShapeDtypeStruct(lagged, F32))
        out_specs.append(vmem)
    batch = min(BATCH, share)
    assert all(rows % batch == 0 for rows in row_steps(share))
    held = share if share % 16 == 0 else channels
    return pl.pallas_call(
        functools.partial(correlation_kernel, offset, earlier, last, sources, share),
        out_shape=out_shape,
        in_specs=in_specs,
        out_specs=out_specs,
        scratch_shapes=[
            pltpu.VMEM((held, pairs * GROUPS * 2 * LANES), F32),
            pltpu.VMEM((pairs * GROUPS, 2 * channels, 2 * LANES), BF16),
            pltpu.VMEM((share, BINS, 2 * channels), BF16),
        ]
        + ([pltpu.VMEM(lagged, F32)] if last else [])
        + [pltpu.SemaphoreType.DMA((share // batch + 1,))],
        compiler_params=pltpu.CompilerParams(vmem_limit_bytes=VMEM_LIMIT),
        input_output_aliases=aliases,
        cost_estimate=pl.CostEstimate(
            flops=2 * share * 2 * BINS * 2 * LANES * pairs * channels,
            bytes_accessed=share * channels * 2 * LANES * 4,
            transcendentals=0,
        ),
        name=f"correlate_{offset}",
    )(*arrays)


def exchanges(ranks):
    return [(2, step) for step in range(ranks)] + [(0, step) for step in range(1, ranks)]


def moved(value, blocks, ranks):
    block_count, rank_count = lax.axis_size("chan"), lax.axis_size("tm")
    pairs = []
    for block in range(block_count):
        for rank in range(rank_count):
            to = ((block + blocks) % block_count) * rank_count + (rank + ranks) % rank_count
            pairs.append((block * rank_count + rank, to))
    return lax.ppermute(value, ("chan", "tm"), pairs)


def swapped(value):
    return lax.ppermute(value, "chan", [(block, block ^ 1) for block in range(lax.axis_size("chan"))])


def shards(traces, plan, dead_channels):
    windows, channels, _ = traces.shape
    ranks = lax.axis_size("tm")
    share = channels // ranks
    assert ranks % 2 == 0
    first_channel = (lax.axis_index("chan") * channels).astype(jnp.int32).reshape(1)
    rank = lax.axis_index("tm").astype(jnp.int32).reshape(1)
    mine, weights, lags = block_spectra(traces, dead_channels, plan, first_channel, windows * ranks)
    received = {}
    for blocks, step in exchanges(ranks):
        received[blocks, step] = moved(mine, blocks, step)
    behind = [received[2, step] for step in range(ranks)]
    own = [mine] + [received[0, step] for step in range(1, ranks)]
    odd = lax.axis_index("chan") % 2 == 1
    run = functools.partial(correlate, rank=rank, weights=weights, lags=lags, own=own, share=share)
    beside = [swapped(jnp.where(odd, behind[0], mine))]
    (kept,) = run(0, far=own)
    later, kept = lax.optimization_barrier((behind[1:], kept))
    behind = behind[:1] + later
    beside += [swapped(jnp.where(odd, far, near)) for far, near in zip(behind[1:], own[1:], strict=True)]
    result, kept = run(2, far=behind, kept=kept, earlier=0)
    (result,) = run(1, far=beside, kept=kept, earlier=2, previous=result, last=True)
    return result


def solution(mesh):
    in_specs = (P("tm", "chan", None), P("chan", None), P())
    out_specs = P("chan", "tm", None, None, None)
    return jax.shard_map(shards, mesh=mesh, in_specs=in_specs, out_specs=out_specs, check_vma=False)
```
